32 devices in a mesh: group: 4 (over z), dp: 2 (over y), tensor: 4 (over x, core).
Axes of the slice: x: 2, y: 2, z: 4, core: 2. Of those that a mesh axis runs over, the one named last changes fastest.
Arguments:
- queries: bfloat16 [1024, 4096], P(('group', 'dp'), 'tensor'), may hold values from -16 to 16
- span_state: bfloat16 [1024, 4096], P(('group', 'dp'), 'tensor'), may hold values from -6 to 6
- neigh_state: bfloat16 [4096, 4096], P(('group', 'dp'), 'tensor'), may hold values from -24 to 24
- counts: int32 [4, 4], P('group'), may hold values from 1 to 2
- norm_gain: float32 [4096], P('tensor'), may hold values from 0.5 to 1.5
- head_gate: float32 [32], P('tensor'), may hold values from 0.3 to 1.5
- out_grad: bfloat16 [1024, 4096], P(('group', 'dp'), 'tensor'), may hold values from -6 to 6
Outputs:
- cross_output: bfloat16 [1024, 4096], P(('group', 'dp'), 'tensor')
- query_grad: bfloat16 [1024, 4096], P(('group', 'dp'), 'tensor')
- span_grad: bfloat16 [1024, 4096], P(('group', 'dp'), 'tensor')
- neighbour_grad: bfloat16 [4096, 4096], P(('group', 'dp'), 'tensor')
- gate_grad: float32 [32], P('tensor')
The draws below stay inside these ranges and needn't reach their ends.
Inputs may be any that keep to these rules, and one draw needn't show every extreme that they name: Slot j of span c holds a retrieved neighbour exactly when j < counts[c].
All inputs are finite; a program needn't handle non-finite values.
Results may differ from the reference program's by a relative error of at most 0.0095.
The reference program's roundings to bfloat16 on the way count: a program that leaves them out, or rounds other values in their place, can miss the bound.
Values may be sent and summed in bfloat16 or wider, within the bound.
A program may use at most 64 MiB of HBM per device.

```python
import math
import jax
import jax.numpy as jnp
from jax import lax

HEADS = 32
HD = 128
CH = 64
NB = 2
NL = 128
HW = 4096
NCH = 4
LEN = 256
SEQS = 4
TOKENS = 1024
NTOK = 4096


def column_scale(lowest, highest):
    fraction = jnp.arange(HW).astype(jnp.float32) / (HW - 1)
    return jnp.exp(jnp.log(lowest) + fraction * (jnp.log(highest) - jnp.log(lowest)))[None, :]


def draw_neigh_state(key, part):
    values = jax.random.normal(jax.random.fold_in(key, 7), (NTOK, HW), jnp.float32)
    values = values * column_scale(0.5, 2.0)
    return jnp.clip(values, -12.0, 12.0).astype(jnp.bfloat16)


def draw_queries(key, part):
    values = jax.random.normal(jax.random.fold_in(key, 9), (TOKENS, HW), jnp.float32)
    return jnp.clip(values, -6.0, 6.0).astype(jnp.bfloat16)


def with_ends(array, own_key, smallest, top_value):
    index_at = [jax.random.randint(jax.random.fold_in(own_key, axis), (), 0, length) for axis, length in enumerate(array.shape)]
    widest = array.shape.index(max(array.shape))
    next_to = index_at[:widest] + [(index_at[widest] + 1) % array.shape[widest]] + index_at[widest + 1:]
    return array.at[tuple(index_at)].set(smallest).at[tuple(next_to)].set(top_value)


def block_levels(rng, shape, pieces, smallest, largest):
    def one(axis_at, blocks):
        draws = jax.random.uniform(jax.random.fold_in(jax.random.fold_in(rng, 6), axis_at), (blocks,), jnp.float32, smallest / len(pieces), largest / len(pieces))
        return jnp.repeat(jnp.exp(draws), shape[axis_at] // blocks).reshape((-1,) + (1,) * (len(shape) - axis_at - 1))

    gain = one(*pieces[0])
    for cut in pieces[1:]:
        gain = gain * one(*cut)
    return gain


def bell_draw(stream_key, shape, scale, reach, pieces=(), held_as=jnp.bfloat16):
    entries = scale * jax.random.normal(stream_key, shape, jnp.float32)
    if pieces:
        entries = entries * block_levels(stream_key, shape, pieces, -0.22, 0.18)
    return jnp.clip(entries, -reach, reach).astype(held_as)


def setup_inputs(seed: int = 0) -> dict:
    key_of = jax.random.split(jax.random.key(seed), 8)
    return {
        "queries": draw_queries(jax.random.fold_in(key_of[7], 71), 0),
        "span_state": bell_draw(key_of[1], (TOKENS, HW), 1.0, 6.0, ((0, 8), (1, 4))),
        "neigh_state": draw_neigh_state(jax.random.fold_in(key_of[7], 71), 0),
        "counts": with_ends(jax.random.randint(key_of[3], (SEQS, NCH), 1, NB + 1), jax.random.fold_in(key_of[3], 1), 1, NB).astype(jnp.int32),
        "norm_gain": jnp.clip(1.0 + 0.1 * jax.random.normal(key_of[4], (HW,), jnp.float32), 0.5, 1.5),
        "head_gate": jnp.clip(0.3 + 1.2 * jax.random.uniform(key_of[5], (HEADS,), jnp.float32) ** block_levels(key_of[5], (HEADS,), ((0, 4),), -0.2, 0.2), 0.3, 1.5),
        "out_grad": bell_draw(key_of[6], (TOKENS, HW), 1.0, 6.0, ((0, 8), (1, 4))),
    }


epsilon = 1e-05
masked_score = -1e+30

def product(form, left, right):
    return jnp.einsum(form, left.astype(jnp.float32), right.astype(jnp.float32))

def encoder_forward(normed, neighbours, contexts):
    slot_count = normed.shape[1]
    spread = jnp.broadcast_to(contexts[:, None], (contexts.shape[0], slot_count) + contexts.shape[1:])
    all_keys = jnp.concatenate([normed, spread], axis=2)
    scores = product('cjqhd,cjkhd->cjhqk', normed, all_keys) / normed.shape[-1]
    powers = jnp.exp(scores)
    weights = powers / lax.optimization_barrier(jnp.sum(powers, axis=-1, keepdims=True))
    rounded = weights.astype(jnp.bfloat16)
    mixture = product('cjhqk,cjkhd->cjqhd', rounded, all_keys)
    encoded = (neighbours.astype(jnp.float32) + mixture).astype(jnp.bfloat16)
    return (encoded, (all_keys, weights, rounded, mixture))

def encoder_backward(grad_encoded, normed, saved):
    all_keys, weights, rounded, mixture = saved
    grad_rounded = grad_encoded.astype(jnp.bfloat16)
    grad_weights = product('cjqhd,cjkhd->cjhqk', grad_rounded, all_keys)
    offset = jnp.moveaxis(lax.optimization_barrier(jnp.sum(grad_encoded * mixture, axis=-1)), -1, 2)[..., None]
    score_grad = (weights * (grad_weights - offset) / normed.shape[-1]).astype(jnp.bfloat16)
    normed_grad = product('cjhqk,cjkhd->cjqhd', score_grad, all_keys)
    key_grad = product('cjhqk,cjqhd->cjkhd', score_grad, normed) + product('cjhqk,cjqhd->cjkhd', rounded, grad_rounded)
    length = normed.shape[2]
    normed_grad = normed_grad + key_grad[:, :, :length]
    context_grad = lax.optimization_barrier(jnp.sum(key_grad[:, :, length:], axis=1))
    return (normed_grad, context_grad)

def cross_attend(blocks, grad_blocks, keys, usable, present, gate_tanh):
    scale = 1.0 / math.sqrt(blocks.shape[-1])
    scores = product('brhd,bmhd->bhrm', blocks, keys) * scale
    scores = jnp.where(usable[:, None, None, :], scores, masked_score)
    highest = lax.optimization_barrier(jnp.max(scores, axis=-1, keepdims=True))
    powers = jnp.exp(scores - highest)
    weights = powers / lax.optimization_barrier(jnp.sum(powers, axis=-1, keepdims=True))
    rounded = weights.astype(jnp.bfloat16)
    attended = product('bhrm,bmhd->brhd', rounded, keys)
    present_mask = present[:, None, None, None]
    attended = jnp.where(present_mask, attended, 0.0)
    output = (gate_tanh[:, None] * attended).astype(jnp.bfloat16)
    grad_output = grad_blocks.astype(jnp.float32)
    gate_term = lax.optimization_barrier(jnp.sum(grad_output * attended, axis=(0, 1, 3)))
    att_grad = jnp.where(present_mask, gate_tanh[:, None] * grad_output, 0.0)
    grad_rounded = att_grad.astype(jnp.bfloat16)
    grad_weights = product('brhd,bmhd->bhrm', grad_rounded, keys)
    offset = jnp.moveaxis(lax.optimization_barrier(jnp.sum(att_grad * attended, axis=-1)), -1, 1)[..., None]
    score_grad = (weights * (grad_weights - offset) * scale).astype(jnp.bfloat16)
    query_grad = product('bhrm,bmhd->brhd', score_grad, keys).astype(jnp.bfloat16)
    key_grad = product('bhrm,brhd->bmhd', score_grad, blocks) + product('bhrm,brhd->bmhd', rounded, grad_rounded)
    return (output, query_grad, key_grad, gate_term)

def reference(queries, span_state, neigh_state, counts, norm_gain, head_gate, out_grad):
    total_spans = SEQS * NCH
    lead = CH - 1

    def shifted(matrix):
        per_sequence = matrix.reshape(SEQS, LEN, HW)
        padding = jnp.zeros((SEQS, lead, HW), matrix.dtype)
        joined = jnp.concatenate([per_sequence[:, lead:], padding], axis=1)
        return joined.reshape(total_spans, CH, HEADS, HD)
    blocks = shifted(queries)
    grad_blocks = shifted(out_grad)
    neighbours = neigh_state.reshape(total_spans, NB, NL, HEADS, HD)
    contexts = span_state.reshape(total_spans, CH, HEADS, HD)
    flat_counts = counts.reshape(total_spans).astype(jnp.int32)
    gains = norm_gain.reshape(HEADS, HD)
    gate_tanh = jnp.tanh(head_gate)

    def one_span(items):
        block, grad_block, neighbour, context, count = items
        neighbour = neighbour[None]
        floats = neighbour.astype(jnp.float32)
        square_sum = lax.optimization_barrier(jnp.sum(floats * floats, axis=(3, 4)))
        inverse = lax.rsqrt(square_sum / (HEADS * HD) + epsilon)[..., None, None]
        scaled = floats * inverse
        normed = (scaled * gains).astype(jnp.bfloat16)
        encoded, saved = encoder_forward(normed, neighbour, context[None])
        keys = encoded.reshape(1, NB * NL, HEADS, HD)
        usable = jnp.repeat(jnp.arange(NB) < count, NL)[None]
        present = (count > 0)[None]
        output, query_grad, key_grad, gate_term = cross_attend(block[None], grad_block[None], keys, usable, present, gate_tanh)
        grad_encoded = key_grad.reshape(1, NB, NL, HEADS, HD)
        normed_grad, context_grad = encoder_backward(grad_encoded, normed, saved)
        gain_grad = normed_grad * gains
        projection = lax.optimization_barrier(jnp.sum(gain_grad * scaled, axis=(3, 4))) / (HEADS * HD)
        neighbour_grad = grad_encoded + inverse * (gain_grad - scaled * projection[..., None, None])
        return (output[0], query_grad[0], context_grad[0].astype(jnp.bfloat16), neighbour_grad[0].astype(jnp.bfloat16), gate_term)
    results = lax.map(one_span, (blocks, grad_blocks, neighbours, contexts, flat_counts))
    out_blocks, grad_rows, context_rows, neighbour_rows, gate_terms = results

    def unshift(stacked):
        per_sequence = stacked.reshape(SEQS, LEN, HW)
        padding = jnp.zeros((SEQS, lead, HW), stacked.dtype)
        joined = jnp.concatenate([padding, per_sequence], axis=1)[:, :LEN]
        return joined.reshape(TOKENS, HW)
    cross_output = unshift(out_blocks)
    query_grad = unshift(grad_rows)
    span_grad = context_rows.reshape(TOKENS, HW)
    neighbour_grad = neighbour_rows.reshape(NTOK, HW)
    gate_grad = (1.0 - gate_tanh * gate_tanh) * lax.optimization_barrier(jnp.sum(gate_terms, axis=0)) / math.sqrt(TOKENS)
    return (cross_output, query_grad, span_grad, neighbour_grad, gate_grad)
```

```python
import functools
import math

import jax
import jax.numpy as jnp
from jax import lax
from jax.experimental import pallas as pl
from jax.experimental.pallas import tpu as pltpu
from jax.sharding import PartitionSpec as P

CH = 64
NB = 2
NL = 128
UNROLL = 2

epsilon = 1e-05
masked_score = -1e30
MESH = pl.DeviceIdType.MESH
F32 = jnp.float32
BF16 = jnp.bfloat16


def nn(left, right):
    return lax.dot_general(left, right, (((1,), (0,)), ((), ())), preferred_element_type=F32)


def nt(left, right):
    return lax.dot_general(left, right, (((1,), (1,)), ((), ())), preferred_element_type=F32)


def tn(left, right):
    return lax.dot_general(left, right, (((0,), (0,)), ((), ())), preferred_element_type=F32)


def kernel(
    sizes,
    q_in, c_in, x_in, counts, gains, gates, og_in,
    out_o, qg_o, sg_o, ng_o, gate_o,
    x_v, c_v, q_v, og_v, halo, qf, ogf, sb, ss, ss_got, inv, pacc, pj, pj_got,
    a_v, ng_v, sg_v, outf, qgf, ret, arr, outb, qgb, gate_buf,
    in_sem, out_sem, halo_s, halo_r, ss_s, ss_r, pj_s, pj_r, ret_s, ret_r, gate_s, gate_r,
):
    n_group, n_dp, n_tensor, heads, hd, rows, seq_spans = sizes
    spans = rows // CH
    lead = CH - 1
    width = heads * hd
    full_width = n_tensor * width
    blocks = spans * NB
    span_rows = NB * NL
    group = lax.axis_index("group")
    dp = lax.axis_index("dp")
    tensor = lax.axis_index("tensor")
    lines = n_group * n_dp
    line = group * n_dp + dp
    first_span = dp * spans
    order = [spans - 1] + list(range(spans - 1))

    def line_peer(d):
        flat = lax.rem(line + d, lines)
        return {"group": flat // n_dp, "dp": lax.rem(flat, n_dp), "tensor": tensor}

    def tensor_peer(d):
        return {"group": group, "dp": dp, "tensor": lax.rem(tensor + d, n_tensor)}

    before = {"group": group, "dp": lax.rem(dp + n_dp - 1, n_dp), "tensor": tensor}
    after = {"group": group, "dp": lax.rem(dp + 1, n_dp), "tensor": tensor}

    def remote(src, dst, send, recv, device):
        return pltpu.make_async_remote_copy(
            src_ref=src, dst_ref=dst, send_sem=send, recv_sem=recv,
            device_id=device, device_id_type=MESH,
        )

    loads = []
    for at, c in enumerate(order):
        piece = pl.ds(c * span_rows, span_rows)
        loads.append(pltpu.make_async_copy(x_in.at[piece], x_v.at[piece], in_sem.at[at]))
    small = [
        pltpu.make_async_copy(q_in, q_v, in_sem.at[spans]),
        pltpu.make_async_copy(og_in, og_v, in_sem.at[spans + 1]),
        pltpu.make_async_copy(c_in, c_v, in_sem.at[spans + 2]),
    ]
    for copy in loads + small:
        copy.start()

    barrier = pltpu.get_barrier_semaphore()
    for d in range(1, n_tensor):
        pl.semaphore_signal(barrier, inc=1, device_id=tensor_peer(d), device_id_type=MESH)
    for d in range(1, lines):
        pl.semaphore_signal(barrier, inc=1, device_id=line_peer(d), device_id_type=MESH)

    def row_sums(value):
        return jnp.sum(value.T, axis=0, keepdims=True)

    def row_spread(line_value):
        return jnp.broadcast_to(line_value, (NL, NL)).T

    for at, c in enumerate(order):
        loads[at].wait()
        for j in range(NB):
            b = c * NB + j
            piece = pl.ds(b * NL, NL)
            total = jnp.zeros((NL, hd), F32)
            for h in range(heads):
                part = x_v[piece, h * hd:(h + 1) * hd].astype(F32)
                total = total + part * part
            ss[b:b + 1, :] = row_sums(total)

    pl.semaphore_wait(barrier, n_tensor - 1 + lines - 1)

    halo_copies = [
        remote(q_in.at[pl.ds(0, CH)], halo.at[0], halo_s.at[0], halo_r.at[0], before),
        remote(og_in.at[pl.ds(0, CH)], halo.at[1], halo_s.at[1], halo_r.at[1], before),
    ]
    ss_copies = [
        remote(ss, ss_got.at[d - 1], ss_s.at[d - 1], ss_r.at[d - 1], tensor_peer(d))
        for d in range(1, n_tensor)
    ]
    for copy in ss_copies + halo_copies:
        copy.start()

    small[0].wait()
    small[1].wait()
    small[2].wait()
    qf[0:rows, :] = q_v[...].astype(F32)
    ogf[0:rows, :] = og_v[...].astype(F32)
    pacc[...] = jnp.zeros_like(pacc)
    gate_buf[line] = jnp.zeros((heads, hd), F32)

    for copy in ss_copies:
        copy.wait()
    square = ss[...]
    for d in range(1, n_tensor):
        square = square + ss_got[d - 1]
    inv[...] = lax.rsqrt(square / full_width + epsilon)
    for b in range(blocks):
        sb[b * NL:(b + 1) * NL, :] = row_spread(inv[b:b + 1, :])

    for copy in halo_copies:
        copy.wait()
    follows = lax.rem(first_span + spans, seq_spans) != 0
    qf[rows:rows + CH, :] = jnp.where(follows, halo[0].astype(F32), 0.0)
    ogf[rows:rows + CH, :] = jnp.where(follows, halo[1].astype(F32), 0.0)

    enc_scale = math.log2(math.e) / hd
    scale = 1.0 / math.sqrt(hd)

    def unit(c, h, usable, present):
        cols = pl.ds(pl.multiple_of(h * hd, hd), hd)
        g = gains[pl.ds(h, 1), :]
        gt = jnp.tanh(jnp.full((1, hd), gates[h], F32))
        context = c_v[c * CH:(c + 1) * CH, cols]
        slots = []
        for j in range(NB):
            base = c * span_rows + j * NL
            x = x_v[base:base + NL, cols].astype(F32)
            normed = (x * sb[base:base + NL, :] * g).astype(BF16)
            keys = jnp.concatenate([normed, context], axis=0)
            powers = jnp.exp2(nt(keys, normed) * enc_scale)
            weights = powers * (1.0 / jnp.sum(powers, axis=0, keepdims=True))
            rounded = weights.astype(BF16)
            encoded = (x + tn(rounded, keys)).astype(BF16)
            slots.append((base, normed, keys, weights, rounded, encoded))
        enc = jnp.concatenate([slot[5] for slot in slots], axis=0)
        at = lead + c * CH
        og = ogf[at:at + CH, cols]
        query = qf[at:at + CH, cols].astype(BF16)
        pair = jnp.concatenate([(gt * og).astype(BF16), query], axis=0)
        both = nt(pair, enc)
        grad_weights = both[:CH]
        scores = jnp.where(usable, both[CH:] * scale, masked_score)
        powers = jnp.exp(scores - jnp.max(scores, axis=1, keepdims=True))
        weights = powers * (present / jnp.sum(powers, axis=1, keepdims=True))
        rounded = weights.astype(BF16)
        offset = jnp.sum(rounded.astype(F32) * grad_weights, axis=1, keepdims=True)
        score_grad = (weights * (grad_weights - offset) * scale).astype(BF16)
        coefficients = jnp.concatenate([rounded, score_grad], axis=0)
        mixed = nn(coefficients, enc)
        attended = mixed[:CH]
        out = gt * attended
        outf[CH + c * CH:2 * CH + c * CH, cols] = out
        qgf[CH + c * CH:2 * CH + c * CH, cols] = mixed[CH:]
        if c == spans - 1:
            ret[0, :, cols] = out.astype(BF16)
            ret[1, :, cols] = mixed[CH:].astype(BF16)
        gate_buf[line, pl.ds(h, 1), :] += jnp.sum(og * attended, axis=0, keepdims=True)
        enc_grad = tn(coefficients, pair)
        span_grad = jnp.zeros((CH, hd), F32)
        for j in range(NB):
            base, normed, keys, weights, rounded, _ = slots[j]
            grad = enc_grad[j * NL:(j + 1) * NL]
            grad_rounded = grad.astype(BF16)
            grad_weights = nt(keys, grad_rounded)
            offset = jnp.sum(rounded.astype(F32) * grad_weights, axis=0, keepdims=True)
            score_grad = (weights * (grad_weights - offset) * (1.0 / hd)).astype(BF16)
            key_grad = nn(
                jnp.concatenate([score_grad, rounded], axis=1),
                jnp.concatenate([normed, grad_rounded], axis=0),
            )
            gained = (tn(score_grad, keys) + key_grad[:NL]) * g
            span_grad = span_grad + key_grad[NL:]
            x = x_v[base:base + NL, cols].astype(F32)
            pacc[base:base + NL, :] += gained * x
            a_v[base:base + NL, cols] = grad + sb[base:base + NL, :] * gained
        sg_v[c * CH:(c + 1) * CH, cols] = span_grad.astype(BF16)

    def project(slot):
        return [
            remote(pj.at[slot], pj_got.at[slot, d - 1], pj_s.at[slot, d - 1],
                   pj_r.at[slot, d - 1], tensor_peer(d))
            for d in range(1, n_tensor)
        ]

    def finish(slot, c):
        total = pj[slot]
        for d in range(1, n_tensor):
            total = total + pj_got[slot, d - 1]
        s = inv[c * NB:(c + 1) * NB, :]
        factor = s * s * s * total / full_width
        for j in range(NB):
            base = c * span_rows + j * NL
            spread = row_spread(factor[j:j + 1, :])
            for h in range(heads):
                cols = slice(h * hd, (h + 1) * hd)
                x = x_v[base:base + NL, cols].astype(F32)
                ng_v[base:base + NL, cols] = (a_v[base:base + NL, cols] - x * spread).astype(BF16)
        piece = pl.ds(c * span_rows, span_rows)
        copy = pltpu.make_async_copy(ng_v.at[piece], ng_o.at[piece], out_sem.at[slot])
        copy.start()
        return copy

    ret_copies = [
        remote(ret.at[i], arr.at[i], ret_s.at[i], ret_r.at[i], after) for i in range(2)
    ]
    pj_copies = []
    for slot, c in enumerate(order):
        index = first_span + c
        count = counts[index // seq_spans, lax.rem(index, seq_spans)]
        usable = lax.broadcasted_iota(jnp.int32, (CH, span_rows), 1) // NL < count
        present = jnp.where(count > 0, 1.0, 0.0).astype(F32)

        def step(i, carry):
            for u in range(UNROLL):
                unit(c, i * UNROLL + u, usable, present)
            return carry

        lax.fori_loop(0, heads // UNROLL, step, 0)
        for j in range(NB):
            base = c * span_rows + j * NL
            pj[slot, j:j + 1, :] = row_sums(pacc[base:base + NL, :])
        copies = project(slot)
        for copy in copies:
            copy.start()
        pj_copies.append(copies)
        if slot == 0:
            for copy in ret_copies:
                copy.start()

    gate_copies = [
        remote(gate_buf.at[line], gate_buf.at[line], gate_s.at[d - 1], gate_r.at[d - 1], line_peer(d))
        for d in range(1, lines)
    ]
    for copy in gate_copies:
        copy.start()
    done = [pltpu.make_async_copy(sg_v, sg_o, out_sem.at[spans])]
    done[0].start()
    for slot in range(spans - 1):
        for copy in pj_copies[slot]:
            copy.wait()
        done.append(finish(slot, order[slot]))
    for copy in ret_copies:
        copy.wait()
    starts = lax.rem(first_span, seq_spans) == 0
    outf[0:CH, :] = jnp.where(starts, 0.0, arr[0].astype(F32))
    qgf[0:CH, :] = jnp.where(starts, 0.0, arr[1].astype(F32))
    outb[...] = outf[1:rows + 1, :].astype(BF16)
    qgb[...] = qgf[1:rows + 1, :].astype(BF16)
    for i, (source, target) in enumerate([(outb, out_o), (qgb, qg_o)]):
        copy = pltpu.make_async_copy(source, target, out_sem.at[spans + 1 + i])
        copy.start()
        done.append(copy)
    for copy in pj_copies[spans - 1]:
        copy.wait()
    done.append(finish(spans - 1, order[spans - 1]))
    for copy in gate_copies:
        copy.wait()
    summed = gate_buf[0]
    for i in range(1, lines):
        summed = summed + gate_buf[i]
    tokens = n_group * n_dp * rows
    for h in range(heads):
        t = jnp.tanh(jnp.full((1, hd), gates[h], F32))
        gate_o[h] = jnp.sum((1.0 - t * t) * summed[h:h + 1, :]) * (1.0 / math.sqrt(tokens))
    for copy in done:
        copy.wait()


def shards(queries, span_state, neigh_state, counts, norm_gain, head_gate, out_grad):
    heads = head_gate.shape[0]
    rows, width = queries.shape
    hd = width // heads
    n_group, n_dp, n_tensor = (lax.axis_size(a) for a in ("group", "dp", "tensor"))
    spans = rows // CH
    blocks = spans * NB
    tokens = neigh_state.shape[0]
    lines = n_group * n_dp
    sizes = (n_group, n_dp, n_tensor, heads, hd, rows, counts.shape[1])
    others = max(1, n_tensor - 1)
    any_space = pl.BlockSpec(memory_space=pl.ANY)
    smem = pl.BlockSpec(memory_space=pltpu.SMEM)
    vmem = pl.BlockSpec(memory_space=pltpu.VMEM)
    dma = pltpu.SemaphoreType.DMA
    return pl.pallas_call(
        functools.partial(kernel, sizes),
        out_shape=(
            jax.ShapeDtypeStruct((rows, width), BF16),
            jax.ShapeDtypeStruct((rows, width), BF16),
            jax.ShapeDtypeStruct((rows, width), BF16),
            jax.ShapeDtypeStruct((tokens, width), BF16),
            jax.ShapeDtypeStruct((heads,), F32),
        ),
        in_specs=[any_space, any_space, any_space, smem, vmem, smem, any_space],
        out_specs=(any_space, any_space, any_space, any_space, smem),
        scratch_shapes=[
            pltpu.VMEM((tokens, width), BF16),
            pltpu.VMEM((rows, width), BF16),
            pltpu.VMEM((rows, width), BF16),
            pltpu.VMEM((rows, width), BF16),
            pltpu.VMEM((2, CH, width), BF16),
            pltpu.VMEM((rows + CH, width), F32),
            pltpu.VMEM((rows + CH, width), F32),
            pltpu.VMEM((tokens, hd), F32),
            pltpu.VMEM((blocks, NL), F32),
            pltpu.VMEM((others, blocks, NL), F32),
            pltpu.VMEM((blocks, NL), F32),
            pltpu.VMEM((tokens, hd), F32),
            pltpu.VMEM((spans, NB, NL), F32),
            pltpu.VMEM((spans, others, NB, NL), F32),
            pltpu.VMEM((tokens, width), F32),
            pltpu.VMEM((tokens, width), BF16),
            pltpu.VMEM((rows, width), BF16),
            pltpu.VMEM((rows + CH, width), F32),
            pltpu.VMEM((rows + CH, width), F32),
            pltpu.VMEM((2, CH, width), BF16),
            pltpu.VMEM((2, CH, width), BF16),
            pltpu.VMEM((rows, width), BF16),
            pltpu.VMEM((rows, width), BF16),
            pltpu.VMEM((lines, heads, hd), F32),
            dma((spans + 3,)),
            dma((spans + 3,)),
            dma((2,)),
            dma((2,)),
            dma((others,)),
            dma((others,)),
            dma((spans, others)),
            dma((spans, others)),
            dma((2,)),
            dma((2,)),
            dma((max(1, lines - 1),)),
            dma((max(1, lines - 1),)),
        ],
        compiler_params=pltpu.CompilerParams(collective_id=0, has_side_effects=True),
    )(queries, span_state, neigh_state, counts, norm_gain.reshape(heads, hd), head_gate, out_grad)


def solution(mesh):
    rows = P(("group", "dp"), "tensor")
    return jax.shard_map(
        shards,
        mesh=mesh,
        in_specs=(rows, rows, rows, P("group", None), P("tensor"), P("tensor"), rows),
        out_specs=(rows, rows, rows, rows, P("tensor")),
        check_vma=False,
    )
```
